256 devices in a mesh: dp: 16 (over y_hi, z), fsdp: 16 (over y_lo, x, core).
Axes of the slice: x: 4, y: 4 (y_hi: 2, y_lo: 2; y = y_hi * 2 + y_lo), z: 8, core: 2. Of those that a mesh axis runs over, the one named last changes fastest.
Arguments:
- item_tokens: bfloat16 [131072, 4096], P(('dp', 'fsdp')), may hold values from -6 to 6
- item_lengths: int32 [1024], P(('dp', 'fsdp')), may hold values from 1 to 128
- item_gain: float32 [4096], replicated, may hold values from 0.1 to 1.9
- user_source: int32 [65536, 1], P(('dp', 'fsdp')), may hold values from 0 to 15; in each aligned block of 256 rows (0 to 255, 256 to 511, ...) at most 24 rows name the same one
- user_slot: int32 [65536], P(('dp', 'fsdp')), may hold values from 0 to 3
- user_lengths: int32 [256], P(('dp', 'fsdp')), may hold values from 1 to 256
- user_gain: float32 [4096], replicated, may hold values from 0.1 to 1.9
- key_weight: bfloat16 [4096, 1024], P('fsdp'), may hold values from -0.09375 to 0.09375
- key_grad: bfloat16 [65536, 1024], P(('dp', 'fsdp')), may hold values from -6 to 6
Outputs:
- keys: bfloat16 [65536, 1024], P(('dp', 'fsdp'))
- weight_grad: float32 [4096, 1024], P('fsdp')
- token_grads: bfloat16 [131072, 4096], P(('dp', 'fsdp'))
The draws below stay inside these ranges and needn't reach their ends.
Inputs may be any that keep to these rules, and one draw needn't show every extreme that they name: `user_source`: among the 256 positions of one device, no source index appears more than 24 times, and in every draw some device reaches 24 for some source.
All inputs are finite; a program needn't handle non-finite values.
Results may differ from the reference program's by a relative error of at most 0.0057.
Values may be sent and summed in bfloat16 or wider, within the bound.
A program may use at most 128 MiB of HBM per device.

```python
import math
import jax
import jax.numpy as jnp
import numpy as np
from jax import lax

D = 4096
KVD = 1024
BLOCK = 128
UL = 256
ITEMS_DEV = 4
SEQ_DEV = 1
U = 256
CAP = 24
ITEMS = 1024
USERS = 65536
SEQS = 256
N_DP = 16
N_FSDP = 16


def set_ends(array, own_key, low, top_value):
    place = [jax.random.randint(jax.random.fold_in(own_key, axis), (), 0, length) for axis, length in enumerate(array.shape)]
    main_axis = array.shape.index(max(array.shape))
    neighbour = place[:main_axis] + [(place[main_axis] + 1) % array.shape[main_axis]] + place[main_axis + 1:]
    return array.at[tuple(place)].set(low).at[tuple(neighbour)].set(top_value)


def level_of(stream_key, shape, split, low, high):
    def one(axis_at, blocks):
        draws = jax.random.uniform(jax.random.fold_in(jax.random.fold_in(stream_key, 6), axis_at), (blocks,), jnp.float32, low / len(split), high / len(split))
        return jnp.repeat(jnp.exp(draws), shape[axis_at] // blocks).reshape((-1,) + (1,) * (len(shape) - axis_at - 1))

    loudness = one(*split[0])
    for cut in split[1:]:
        loudness = loudness * one(*cut)
    return loudness


def assign_block(stream_key, own, number, rows, count, top, limit, skew):
    ranking = jax.random.permutation(stream_key, count)
    crowded, ordinary = load_shares(count, rows * top, limit, skew, True), load_shares(count, rows * top, limit, skew, False)
    places = jnp.arange(count)

    def named(lengths, rotation):
        used = int((lengths > 0).sum())
        fixed = max(1, used // 4)
        shifted = fixed + (places - fixed + rotation * (used - fixed)) % max(1, count - fixed)
        return jnp.zeros((count,), jnp.int32).at[ranking[jnp.where(places < fixed, places, shifted)]].set(jnp.asarray(lengths, jnp.int32))

    lengths = jnp.where(number % 4 == 0, named(crowded, number // 4), named(ordinary, number - number // 4 - 1))
    mixed = jax.random.permutation(jax.random.fold_in(own, 3), count)
    source_of, taker = mixed[0:count // 2 * 2:2], mixed[1:count // 2 * 2:2]
    slack = jnp.minimum(lengths[source_of] - 1, limit - lengths[taker]) // 2
    slack = jnp.where((source_of == ranking[0]) | (taker == ranking[0]) | (lengths[taker] == 0), 0, jnp.maximum(slack, 0))
    shifted = jax.random.randint(jax.random.fold_in(own, 4), (count // 2,), 0, 1 << 20) % (slack + 1)
    lengths = lengths.at[source_of].add(-shifted).at[taker].add(shifted)
    labels = jnp.searchsorted(jnp.cumsum(lengths), jnp.arange(rows * top), side="right").astype(jnp.int32)
    table = labels.reshape(top, rows).T
    table = table[jax.random.permutation(jax.random.fold_in(own, 1), rows)]
    rotation = jax.random.randint(jax.random.fold_in(own, 2), (rows, 1), 0, top)
    return jnp.take_along_axis(table, (jnp.arange(top)[None, :] + rotation) % top, axis=1)


def load_shares(amount, total, most, skew, full):
    loads = [(1 << 20) // math.isqrt(standing ** skew) + 1 for standing in range(1, amount + 1)]
    largest = most if full else min(most, max(-(-total // amount), total * loads[0] // sum(loads)))
    least = 1 if total - largest >= amount - 1 else 0
    given, rest = [largest] + [least] * (amount - 1), total - largest - least * (amount - 1)
    while rest > 0:
        movable = [i for i in range(1, amount) if given[i] < largest] or [i for i in range(1, amount) if given[i] < most]
        whole, remaining = sum([loads[i] for i in movable]), rest
        for i in movable:
            addition = min(most - given[i], max(1, remaining * loads[i] // whole), rest)
            given[i] = given[i] + addition
            rest = rest - addition
    return np.array(given)


def scatter_about(key, extent, width, most, shards=(), held_as=jnp.bfloat16):
    level = level_of(key, extent, shards, -0.22, 0.18) if shards else 1.0
    array = jax.random.normal(key, extent, jnp.float32) * width * level
    return jnp.minimum(jnp.maximum(array, -most), most).astype(held_as)


def setup_inputs(seed: int = 0) -> dict:
    key_list = jax.random.split(jax.random.key(seed), 10)
    item_tokens = scatter_about(key_list[0], (ITEMS * BLOCK, D), 1.0, 6.0, ((0, 256),))
    item_lengths = set_ends(jax.random.randint(key_list[1], (ITEMS,), 1, BLOCK + 1), jax.random.fold_in(key_list[1], 1), 1, BLOCK).astype(jnp.int32)
    item_gain = jnp.clip(1.0 + 0.18 * jax.random.normal(key_list[2], (D,), jnp.float32), 0.1, 1.9)
    user_source_keys = jax.random.split(jax.random.fold_in(key_list[3], 1), USERS // U)
    user_source_turns = jax.random.permutation(jax.random.fold_in(key_list[3], 3), USERS // U)
    user_source = jax.vmap(lambda own, number: assign_block(jax.random.fold_in(key_list[3], 2), own, number, U, N_DP, 1, CAP, 2))(user_source_keys, user_source_turns).reshape((USERS, 1))
    user_slot = set_ends(jax.random.randint(key_list[4], (USERS,), 0, ITEMS_DEV), jax.random.fold_in(key_list[4], 1), 0, ITEMS_DEV - 1).astype(jnp.int32)
    user_lengths = set_ends(jax.random.randint(key_list[5], (SEQS,), 1, UL + 1), jax.random.fold_in(key_list[5], 1), 1, UL).astype(jnp.int32)
    user_gain = jnp.clip(1.0 + 0.18 * jax.random.normal(key_list[6], (D,), jnp.float32), 0.1, 1.9)
    key_weight = scatter_about(key_list[7], (D, KVD), D ** -0.5, 0.09375, ((0, 16),))
    key_grad = scatter_about(key_list[8], (USERS, KVD), 1.0, 6.0, ((0, 256),))
    return dict(item_tokens=item_tokens, item_lengths=item_lengths, item_gain=item_gain, user_source=user_source, user_slot=user_slot, user_lengths=user_lengths, user_gain=user_gain, key_weight=key_weight, key_grad=key_grad)


EPS = 1e-05

def rms_scale(vector, gain_row):
    return vector * lax.rsqrt(lax.optimization_barrier(jnp.mean(vector * vector, axis=-1, keepdims=True)) + EPS) * gain_row

def pool_items(token_block, valid_mask, item_sizes, gain_row):
    normed = rms_scale(token_block, gain_row)
    return lax.optimization_barrier(jnp.sum(normed * valid_mask[:, :, None], axis=1)) / item_sizes[:, None]

def item_masks(length_block, block_rows):
    valid_mask = (lax.broadcasted_iota(jnp.int32, (length_block.shape[0], block_rows), 1) < length_block[:, None]).astype(jnp.float32)
    return (valid_mask, length_block.astype(jnp.float32))

def reference(item_tokens, item_lengths, item_gain, user_source, user_slot, user_lengths, user_gain, key_weight, key_grad):
    device_count = N_DP * N_FSDP
    row_count = SEQ_DEV * UL
    stacked_tokens = item_tokens.reshape(device_count, ITEMS_DEV, BLOCK, D)
    length_rows = item_lengths.reshape(device_count, ITEMS_DEV)

    def pool_device(inputs_pair):
        token_block, length_block = inputs_pair
        valid_mask, item_sizes = item_masks(length_block, BLOCK)
        return pool_items(token_block.astype(jnp.float32), valid_mask, item_sizes, item_gain).astype(jnp.bfloat16)
    item_emb = lax.map(pool_device, (stacked_tokens, length_rows)).reshape(ITEMS, D)
    position = jnp.arange(USERS, dtype=jnp.int32)
    device_of = position // row_count
    fsdp_index = device_of % N_FSDP
    item_index = ((user_source[:, 0] * N_FSDP + fsdp_index) * ITEMS_DEV + user_slot).astype(jnp.int32)
    seq_of = position // UL
    alive_all = position % UL < user_lengths[seq_of]
    index_rows = item_index.reshape(device_count, row_count)
    alive_rows = alive_all.reshape(device_count, row_count)
    grad_rows = key_grad.reshape(device_count, row_count, KVD)

    def normalize(vector):
        return rms_scale(vector, user_gain)

    def scan_step(carry, block_in):
        weight_acc, grad_acc = carry
        index_block, alive_block, key_block = block_in
        gathered = jnp.take(item_emb, index_block, axis=0)
        embedded = jnp.where(alive_block[:, None], gathered, jnp.zeros_like(gathered))
        scaled, norm_back = jax.vjp(normalize, embedded.astype(jnp.float32))
        hidden = scaled.astype(jnp.bfloat16)
        key_rows = jnp.dot(hidden, key_weight, preferred_element_type=jnp.float32).astype(jnp.bfloat16)
        hidden_grad = lax.dot_general(key_block, key_weight, (((1,), (1,)), ((), ())), preferred_element_type=jnp.float32)
        embed_grad, = norm_back(hidden_grad)
        pos_grad = jnp.where(alive_block[:, None], embed_grad, jnp.zeros_like(embed_grad)).astype(jnp.bfloat16)
        columns = lax.dot_general(hidden, key_block, (((0,), (0,)), ((), ())), preferred_element_type=jnp.float32)
        weight_acc = weight_acc + columns
        grad_acc = grad_acc + jax.ops.segment_sum(pos_grad.astype(jnp.float32), index_block, num_segments=ITEMS)
        return ((weight_acc, grad_acc), key_rows)
    start_carry = (jnp.zeros((D, KVD), jnp.float32), jnp.zeros((ITEMS, D), jnp.float32))
    (weight_grad, item_grad), key_out = lax.scan(scan_step, start_carry, (index_rows, alive_rows, grad_rows))
    keys = key_out.reshape(USERS, KVD)
    grad_blocks = item_grad.reshape(device_count, ITEMS_DEV, D)

    def token_grad(inputs_triple):
        token_block, length_block, grad_block = inputs_triple
        valid_mask, item_sizes = item_masks(length_block, BLOCK)

        def pooling(tokens_float):
            return pool_items(tokens_float, valid_mask, item_sizes, item_gain)
        pooled, pool_back = jax.vjp(pooling, token_block.astype(jnp.float32))
        result, = pool_back(grad_block.astype(pooled.dtype))
        return result.astype(jnp.bfloat16)
    token_grads = lax.map(token_grad, (stacked_tokens, length_rows, grad_blocks)).reshape(ITEMS * BLOCK, D)
    return (keys, weight_grad, token_grads)
```

```python
import jax
import jax.numpy as jnp
from jax import lax
from jax.sharding import PartitionSpec as P

EPS = 1e-05


def rms_scale(vector, gain_row):
    return vector * lax.rsqrt(jnp.mean(vector * vector, axis=-1, keepdims=True) + EPS) * gain_row


def pool_items(token_block, valid_mask, item_sizes, gain_row):
    normed = rms_scale(token_block, gain_row)
    return jnp.sum(normed * valid_mask[:, :, None], axis=1) / item_sizes[:, None]


def local(
    item_tokens,
    item_lengths,
    item_gain,
    user_source,
    user_slot,
    user_lengths,
    user_gain,
    key_weight,
    key_grad,
):
    item_count = item_lengths.shape[0]
    block_rows = item_tokens.shape[0] // item_count
    model_width = item_tokens.shape[1]
    group_count = lax.axis_size("dp")
    stacked_tokens = item_tokens.reshape(item_count, block_rows, model_width)
    valid_mask = (
        lax.broadcasted_iota(jnp.int32, (item_count, block_rows), 1) < item_lengths[:, None]
    ).astype(jnp.float32)
    item_sizes = item_lengths.astype(jnp.float32)

    def pooling(tokens_float):
        return pool_items(tokens_float, valid_mask, item_sizes, item_gain)

    pooled, pool_back = jax.vjp(pooling, stacked_tokens.astype(jnp.float32))
    item_emb = pooled.astype(jnp.bfloat16)
    weights = lax.all_gather(key_weight, "fsdp", axis=0, tiled=True)
    grads_all = lax.all_gather(key_grad, "fsdp", axis=0, tiled=True)
    row_count = user_slot.shape[0]
    source = user_source[:, 0]
    seq_count = user_lengths.shape[0]
    seq_rows = row_count // seq_count
    alive_mask = (
        lax.broadcasted_iota(jnp.int32, (seq_count, seq_rows), 1) < user_lengths[:, None]
    ).reshape(row_count, 1)
    table = lax.all_to_all(
        jnp.broadcast_to(item_emb[None], (group_count, item_count, model_width)),
        "dp",
        split_axis=0,
        concat_axis=0,
        tiled=True,
    ).reshape(group_count * item_count, model_width)
    item_index = source * item_count + user_slot
    pick = (
        (item_index[:, None] == lax.broadcasted_iota(jnp.int32, (row_count, group_count * item_count), 1))
        & alive_mask
    ).astype(jnp.bfloat16)
    embedded = jnp.dot(pick, table, preferred_element_type=jnp.float32).astype(jnp.bfloat16)

    def normalize(vector):
        return rms_scale(vector, user_gain)

    scaled, norm_back = jax.vjp(normalize, embedded.astype(jnp.float32))
    hidden = scaled.astype(jnp.bfloat16)
    key_rows = jnp.dot(hidden, weights, preferred_element_type=jnp.float32).astype(jnp.bfloat16)
    hidden_grad = lax.dot_general(
        key_grad, weights, (((1,), (1,)), ((), ())), preferred_element_type=jnp.float32
    )
    (embed_grad,) = norm_back(hidden_grad)
    pos_grad = jnp.where(alive_mask, embed_grad, jnp.zeros_like(embed_grad)).astype(jnp.bfloat16)
    hidden_cols = lax.all_to_all(hidden, "fsdp", split_axis=1, concat_axis=0, tiled=True)
    weight_part = lax.dot_general(
        hidden_cols, grads_all, (((0,), (0,)), ((), ())), preferred_element_type=jnp.float32
    )
    weight_rows = weight_part.shape[0]
    reduced = jnp.sum(
        lax.all_to_all(weight_part, "dp", split_axis=0, concat_axis=0, tiled=True).reshape(
            group_count, weight_rows // group_count, weight_part.shape[1]
        ),
        axis=0,
    )
    weight_grad = lax.all_to_all(
        jnp.broadcast_to(reduced[None], (group_count,) + reduced.shape),
        "dp",
        split_axis=0,
        concat_axis=0,
        tiled=True,
    ).reshape(weight_rows, weight_part.shape[1])
    item_part = lax.dot_general(
        pick, pos_grad, (((0,), (0,)), ((), ())), preferred_element_type=jnp.float32
    ).reshape(group_count, item_count, model_width)
    item_grad = jnp.sum(
        lax.all_to_all(item_part, "dp", split_axis=0, concat_axis=0, tiled=True), axis=0
    )
    (tokens_back,) = pool_back(item_grad)
    token_grads = tokens_back.reshape(item_count * block_rows, model_width).astype(jnp.bfloat16)
    return (key_rows, weight_grad, token_grads)


def solution(mesh):
    in_specs = (
        P(("dp", "fsdp"), None),
        P(("dp", "fsdp")),
        P(),
        P(("dp", "fsdp"), None),
        P(("dp", "fsdp")),
        P(("dp", "fsdp")),
        P(),
        P("fsdp", None),
        P(("dp", "fsdp"), None),
    )
    out_specs = (P(("dp", "fsdp"), None), P("fsdp", None), P(("dp", "fsdp"), None))
    return jax.shard_map(local, mesh=mesh, in_specs=in_specs, out_specs=out_specs, check_vma=False)
```

```python
import jax
import jax.numpy as jnp
from jax import lax
from jax.sharding import PartitionSpec as P

EPS = 1e-05


def rms_scale(vector, gain_row):
    return vector * lax.rsqrt(jnp.mean(vector * vector, axis=-1, keepdims=True) + EPS) * gain_row


def pool_items(token_block, valid_mask, item_sizes, gain_row):
    normed = rms_scale(token_block, gain_row)
    return jnp.sum(normed * valid_mask[:, :, None], axis=1) / item_sizes[:, None]


def local(
    item_tokens,
    item_lengths,
    item_gain,
    user_source,
    user_slot,
    user_lengths,
    user_gain,
    key_weight,
    key_grad,
):
    item_count = item_lengths.shape[0]
    block_rows = item_tokens.shape[0] // item_count
    model_width = item_tokens.shape[1]
    group_count = lax.axis_size("dp")
    stacked_tokens = item_tokens.reshape(item_count, block_rows, model_width)
    valid_mask = (
        lax.broadcasted_iota(jnp.int32, (item_count, block_rows), 1) < item_lengths[:, None]
    ).astype(jnp.float32)
    item_sizes = item_lengths.astype(jnp.float32)

    def pooling(tokens_float):
        return pool_items(tokens_float, valid_mask, item_sizes, item_gain)

    pooled, pool_back = jax.vjp(pooling, stacked_tokens.astype(jnp.float32))
    item_emb = pooled.astype(jnp.bfloat16)
    weights = lax.all_gather(key_weight, "fsdp", axis=0, tiled=True)
    part_count = 2
    part_width = key_grad.shape[1] // part_count
    grad_parts = [
        lax.all_gather(key_grad[:, k * part_width : (k + 1) * part_width], "fsdp", axis=0, tiled=True)
        for k in range(part_count)
    ]
    row_count = user_slot.shape[0]
    source = user_source[:, 0]
    seq_count = user_lengths.shape[0]
    seq_rows = row_count // seq_count
    alive_mask = (
        lax.broadcasted_iota(jnp.int32, (seq_count, seq_rows), 1) < user_lengths[:, None]
    ).reshape(row_count, 1)
    table = lax.all_to_all(
        jnp.broadcast_to(item_emb[None], (group_count, item_count, model_width)),
        "dp",
        split_axis=0,
        concat_axis=0,
        tiled=True,
    ).reshape(group_count * item_count, model_width)
    item_index = source * item_count + user_slot
    pick = (
        (item_index[:, None] == lax.broadcasted_iota(jnp.int32, (row_count, group_count * item_count), 1))
        & alive_mask
    ).astype(jnp.bfloat16)
    embedded = jnp.dot(pick, table, preferred_element_type=jnp.float32).astype(jnp.bfloat16)

    def normalize(vector):
        return rms_scale(vector, user_gain)

    scaled, norm_back = jax.vjp(normalize, embedded.astype(jnp.float32))
    hidden = scaled.astype(jnp.bfloat16)
    key_rows = jnp.dot(hidden, weights, preferred_element_type=jnp.float32).astype(jnp.bfloat16)
    hidden_grad = lax.dot_general(
        key_grad, weights, (((1,), (1,)), ((), ())), preferred_element_type=jnp.float32
    )
    (embed_grad,) = norm_back(hidden_grad)
    pos_grad = jnp.where(alive_mask, embed_grad, jnp.zeros_like(embed_grad)).astype(jnp.bfloat16)
    item_part = lax.dot_general(
        pick, pos_grad, (((0,), (0,)), ((), ())), preferred_element_type=jnp.float32
    ).reshape(group_count, item_count, model_width)
    item_grad = jnp.sum(
        lax.all_to_all(item_part, "dp", split_axis=0, concat_axis=0, tiled=True), axis=0
    )
    item_grad, grad_parts[0] = lax.optimization_barrier((item_grad, grad_parts[0]))
    fsdp_count = lax.axis_size("fsdp")
    hidden_split = hidden.reshape(row_count, fsdp_count, model_width // fsdp_count).transpose(1, 0, 2)
    hidden_cols = lax.all_to_all(hidden_split, "fsdp", split_axis=0, concat_axis=0, tiled=True).reshape(
        fsdp_count * row_count, model_width // fsdp_count
    )
    weight_rows = hidden_cols.shape[1]
    pieces = []
    for grads_all in grad_parts:
        weight_part = lax.dot_general(
            hidden_cols, grads_all, (((0,), (0,)), ((), ())), preferred_element_type=jnp.float32
        )
        reduced = jnp.sum(
            lax.all_to_all(weight_part, "dp", split_axis=0, concat_axis=0, tiled=True).reshape(
                group_count, weight_rows // group_count, part_width
            ),
            axis=0,
        )
        pieces.append(
            lax.all_to_all(
                jnp.broadcast_to(reduced[None], (group_count,) + reduced.shape),
                "dp",
                split_axis=0,
                concat_axis=0,
                tiled=True,
            ).reshape(weight_rows, part_width)
        )
    weight_grad = jnp.concatenate(pieces, axis=1)
    (tokens_back,) = pool_back(item_grad)
    token_grads = tokens_back.reshape(item_count * block_rows, model_width).astype(jnp.bfloat16)
    return (key_rows, weight_grad, token_grads)


def solution(mesh):
    in_specs = (
        P(("dp", "fsdp"), None),
        P(("dp", "fsdp")),
        P(),
        P(("dp", "fsdp"), None),
        P(("dp", "fsdp")),
        P(("dp", "fsdp")),
        P(),
        P("fsdp", None),
        P(("dp", "fsdp"), None),
    )
    out_specs = (P(("dp", "fsdp"), None), P("fsdp", None), P(("dp", "fsdp"), None))
    return jax.shard_map(local, mesh=mesh, in_specs=in_specs, out_specs=out_specs, check_vma=False)
```

```python
import jax
import jax.numpy as jnp
from jax import lax
from jax.sharding import PartitionSpec as P

EPS = 1e-05


def rms_scale(vector, gain_row):
    return vector * lax.rsqrt(jnp.mean(vector * vector, axis=-1, keepdims=True) + EPS) * gain_row


def pool_items(token_block, valid_mask, item_sizes, gain_row):
    normed = rms_scale(token_block, gain_row)
    return jnp.sum(normed * valid_mask[:, :, None], axis=1) / item_sizes[:, None]


def local(
    item_tokens,
    item_lengths,
    item_gain,
    user_source,
    user_slot,
    user_lengths,
    user_gain,
    key_weight,
    key_grad,
):
    item_count = item_lengths.shape[0]
    block_rows = item_tokens.shape[0] // item_count
    model_width = item_tokens.shape[1]
    group_count = lax.axis_size("dp")
    stacked_tokens = item_tokens.reshape(item_count, block_rows, model_width)
    valid_mask = (
        lax.broadcasted_iota(jnp.int32, (item_count, block_rows), 1) < item_lengths[:, None]
    ).astype(jnp.float32)
    item_sizes = item_lengths.astype(jnp.float32)

    def pooling(tokens_float):
        return pool_items(tokens_float, valid_mask, item_sizes, item_gain)

    pooled, pool_back = jax.vjp(pooling, stacked_tokens.astype(jnp.float32))
    item_emb = pooled.astype(jnp.bfloat16)
    fsdp_count = lax.axis_size("fsdp")
    shard_rows = key_weight.shape[0]
    gathered = lax.all_gather(
        jnp.concatenate([key_weight, key_grad], axis=0), "fsdp", axis=0, tiled=False
    )
    weights = gathered[:, :shard_rows].reshape(fsdp_count * shard_rows, key_weight.shape[1])
    grads_all = gathered[:, shard_rows:].reshape(fsdp_count * key_grad.shape[0], key_grad.shape[1])
    row_count = user_slot.shape[0]
    source = user_source[:, 0]
    seq_count = user_lengths.shape[0]
    seq_rows = row_count // seq_count
    alive_mask = (
        lax.broadcasted_iota(jnp.int32, (seq_count, seq_rows), 1) < user_lengths[:, None]
    ).reshape(row_count, 1)
    table = lax.all_to_all(
        jnp.broadcast_to(item_emb[None], (group_count, item_count, model_width)),
        "dp",
        split_axis=0,
        concat_axis=0,
        tiled=True,
    ).reshape(group_count * item_count, model_width)
    item_index = source * item_count + user_slot
    pick = (
        (item_index[:, None] == lax.broadcasted_iota(jnp.int32, (row_count, group_count * item_count), 1))
        & alive_mask
    ).astype(jnp.bfloat16)
    embedded = jnp.dot(pick, table, preferred_element_type=jnp.float32).astype(jnp.bfloat16)

    def normalize(vector):
        return rms_scale(vector, user_gain)

    scaled, norm_back = jax.vjp(normalize, embedded.astype(jnp.float32))
    hidden = scaled.astype(jnp.bfloat16)
    key_rows = jnp.dot(hidden, weights, preferred_element_type=jnp.float32).astype(jnp.bfloat16)
    hidden_grad = lax.dot_general(
        key_grad, weights, (((1,), (1,)), ((), ())), preferred_element_type=jnp.float32
    )
    (embed_grad,) = norm_back(hidden_grad)
    pos_grad = jnp.where(alive_mask, embed_grad, jnp.zeros_like(embed_grad)).astype(jnp.bfloat16)
    hidden_split = hidden.reshape(row_count, fsdp_count, model_width // fsdp_count).transpose(1, 0, 2)
    hidden_cols = lax.all_to_all(hidden_split, "fsdp", split_axis=0, concat_axis=0, tiled=True).reshape(
        fsdp_count * row_count, model_width // fsdp_count
    )
    weight_part = lax.dot_general(
        hidden_cols, grads_all, (((0,), (0,)), ((), ())), preferred_element_type=jnp.float32
    )
    weight_rows, weight_cols = weight_part.shape
    item_part = lax.dot_general(
        pick, pos_grad, (((0,), (0,)), ((), ())), preferred_element_type=jnp.float32
    )
    item_rows = item_count * model_width // weight_cols
    outgoing = jnp.concatenate(
        [
            weight_part.reshape(group_count, weight_rows // group_count, weight_cols),
            item_part.reshape(group_count, item_rows, weight_cols),
        ],
        axis=1,
    )
    arrived = jnp.sum(lax.all_to_all(outgoing, "dp", split_axis=0, concat_axis=0, tiled=True), axis=0)
    reduced = arrived[: weight_rows // group_count]
    item_grad = arrived[weight_rows // group_count :].reshape(item_count, model_width)
    weight_grad = lax.all_to_all(
        jnp.broadcast_to(reduced[None], (group_count,) + reduced.shape),
        "dp",
        split_axis=0,
        concat_axis=0,
        tiled=True,
    ).reshape(weight_rows, weight_cols)
    (tokens_back,) = pool_back(item_grad)
    token_grads = tokens_back.reshape(item_count * block_rows, model_width).astype(jnp.bfloat16)
    return (key_rows, weight_grad, token_grads)


def solution(mesh):
    in_specs = (
        P(("dp", "fsdp"), None),
        P(("dp", "fsdp")),
        P(),
        P(("dp", "fsdp"), None),
        P(("dp", "fsdp")),
        P(("dp", "fsdp")),
        P(),
        P("fsdp", None),
        P(("dp", "fsdp"), None),
    )
    out_specs = (P(("dp", "fsdp"), None), P("fsdp", None), P(("dp", "fsdp"), None))
    return jax.shard_map(local, mesh=mesh, in_specs=in_specs, out_specs=out_specs, check_vma=False)
```

```python
import jax
import jax.numpy as jnp
from jax import lax
from jax.sharding import PartitionSpec as P

EPS = 1e-05


def rms_scale(vector, gain_row):
    return vector * lax.rsqrt(jnp.mean(vector * vector, axis=-1, keepdims=True) + EPS) * gain_row


def pool_items(token_block, valid_mask, item_sizes, gain_row):
    normed = rms_scale(token_block, gain_row)
    return jnp.sum(normed * valid_mask[:, :, None], axis=1) / item_sizes[:, None]


def local(
    item_tokens,
    item_lengths,
    item_gain,
    user_source,
    user_slot,
    user_lengths,
    user_gain,
    key_weight,
    key_grad,
):
    item_count = item_lengths.shape[0]
    block_rows = item_tokens.shape[0] // item_count
    model_width = item_tokens.shape[1]
    group_count = lax.axis_size("dp")
    stacked_tokens = item_tokens.reshape(item_count, block_rows, model_width)
    valid_mask = (
        lax.broadcasted_iota(jnp.int32, (item_count, block_rows), 1) < item_lengths[:, None]
    ).astype(jnp.float32)
    item_sizes = item_lengths.astype(jnp.float32)

    def pooling(tokens_float):
        return pool_items(tokens_float, valid_mask, item_sizes, item_gain)

    pooled, pool_back = jax.vjp(pooling, stacked_tokens.astype(jnp.float32))
    item_emb = pooled.astype(jnp.bfloat16)
    fsdp_count = lax.axis_size("fsdp")
    shard_rows = key_weight.shape[0]
    gathered = lax.all_gather(
        jnp.concatenate([key_weight, key_grad], axis=0), "fsdp", axis=0, tiled=False
    )
    weights = gathered[:, :shard_rows].reshape(fsdp_count * shard_rows, key_weight.shape[1])
    grads_all = gathered[:, shard_rows:].reshape(fsdp_count * key_grad.shape[0], key_grad.shape[1])
    row_count = user_slot.shape[0]
    source = user_source[:, 0]
    seq_count = user_lengths.shape[0]
    seq_rows = row_count // seq_count
    alive_mask = (
        lax.broadcasted_iota(jnp.int32, (seq_count, seq_rows), 1) < user_lengths[:, None]
    ).reshape(row_count, 1)
    table = lax.all_to_all(
        jnp.broadcast_to(item_emb[None], (group_count, item_count, model_width)),
        "dp",
        split_axis=0,
        concat_axis=0,
        tiled=True,
    ).reshape(group_count * item_count, model_width)
    item_index = source * item_count + user_slot
    pick = (
        (item_index[:, None] == lax.broadcasted_iota(jnp.int32, (row_count, group_count * item_count), 1))
        & alive_mask
    ).astype(jnp.bfloat16)
    embedded = jnp.dot(pick, table, preferred_element_type=jnp.float32).astype(jnp.bfloat16)

    def normalize(vector):
        return rms_scale(vector, user_gain)

    scaled, norm_back = jax.vjp(normalize, embedded.astype(jnp.float32))
    hidden = scaled.astype(jnp.bfloat16)
    hidden_split = hidden.reshape(row_count, fsdp_count, model_width // fsdp_count).transpose(1, 0, 2)
    hidden_cols = lax.all_to_all(hidden_split, "fsdp", split_axis=0, concat_axis=0, tiled=True).reshape(
        fsdp_count * row_count, model_width // fsdp_count
    )
    key_rows = jnp.dot(hidden, weights, preferred_element_type=jnp.float32).astype(jnp.bfloat16)
    hidden_grad = lax.dot_general(
        key_grad, weights, (((1,), (1,)), ((), ())), preferred_element_type=jnp.float32
    )
    (embed_grad,) = norm_back(hidden_grad)
    pos_grad = jnp.where(alive_mask, embed_grad, jnp.zeros_like(embed_grad)).astype(jnp.bfloat16)
    hidden_cols, weights, grads_all = lax.optimization_barrier((hidden_cols, weights, grads_all))
    weight_part = lax.dot_general(
        hidden_cols, grads_all, (((0,), (0,)), ((), ())), preferred_element_type=jnp.float32
    )
    weight_rows, weight_cols = weight_part.shape
    item_part = lax.dot_general(
        pick, pos_grad, (((0,), (0,)), ((), ())), preferred_element_type=jnp.float32
    )
    item_rows = item_count * model_width // weight_cols
    outgoing = jnp.concatenate(
        [
            weight_part.reshape(group_count, weight_rows // group_count, weight_cols),
            item_part.reshape(group_count, item_rows, weight_cols),
        ],
        axis=1,
    ).astype(jnp.bfloat16)
    arrived = jnp.sum(
        lax.all_to_all(outgoing, "dp", split_axis=0, concat_axis=0, tiled=True).astype(jnp.float32), axis=0
    )
    reduced = arrived[: weight_rows // group_count]
    item_grad = arrived[weight_rows // group_count :].reshape(item_count, model_width)
    weight_grad = lax.all_to_all(
        jnp.broadcast_to(reduced[None], (group_count,) + reduced.shape),
        "dp",
        split_axis=0,
        concat_axis=0,
        tiled=True,
    ).reshape(weight_rows, weight_cols)
    (tokens_back,) = pool_back(item_grad)
    token_grads = tokens_back.reshape(item_count * block_rows, model_width).astype(jnp.bfloat16)
    return (key_rows, weight_grad, token_grads)


def solution(mesh):
    in_specs = (
        P(("dp", "fsdp"), None),
        P(("dp", "fsdp")),
        P(),
        P(("dp", "fsdp"), None),
        P(("dp", "fsdp")),
        P(("dp", "fsdp")),
        P(),
        P("fsdp", None),
        P(("dp", "fsdp"), None),
    )
    out_specs = (P(("dp", "fsdp"), None), P("fsdp", None), P(("dp", "fsdp"), None))
    return jax.shard_map(local, mesh=mesh, in_specs=in_specs, out_specs=out_specs, check_vma=False)
```

```python
import jax
import jax.numpy as jnp
from jax import lax
from jax.sharding import PartitionSpec as P

EPS = 1e-05


def rms_scale(vector, gain_row):
    return vector * lax.rsqrt(jnp.mean(vector * vector, axis=-1, keepdims=True) + EPS) * gain_row


def pool_items(token_block, valid_mask, item_sizes, gain_row):
    normed = rms_scale(token_block, gain_row)
    return jnp.sum(normed * valid_mask[:, :, None], axis=1) / item_sizes[:, None]


def local(
    item_tokens,
    item_lengths,
    item_gain,
    user_source,
    user_slot,
    user_lengths,
    user_gain,
    key_weight,
    key_grad,
):
    item_count = item_lengths.shape[0]
    block_rows = item_tokens.shape[0] // item_count
    model_width = item_tokens.shape[1]
    group_count = lax.axis_size("dp")
    stacked_tokens = item_tokens.reshape(item_count, block_rows, model_width)
    valid_mask = (
        lax.broadcasted_iota(jnp.int32, (item_count, block_rows), 1) < item_lengths[:, None]
    ).astype(jnp.float32)
    item_sizes = item_lengths.astype(jnp.float32)

    def pooling(tokens_float):
        return pool_items(tokens_float, valid_mask, item_sizes, item_gain)

    pooled, pool_back = jax.vjp(pooling, stacked_tokens.astype(jnp.float32))
    item_emb = pooled.astype(jnp.bfloat16)
    fsdp_count = lax.axis_size("fsdp")
    shard_rows = key_weight.shape[0]
    gathered = lax.all_gather(
        jnp.concatenate([key_weight, key_grad], axis=0), "fsdp", axis=0, tiled=False
    )
    row_count = user_slot.shape[0]
    source = user_source[:, 0]
    seq_count = user_lengths.shape[0]
    seq_rows = row_count // seq_count
    alive_mask = (
        lax.broadcasted_iota(jnp.int32, (seq_count, seq_rows), 1) < user_lengths[:, None]
    ).reshape(row_count, 1)
    table = lax.all_to_all(
        jnp.broadcast_to(item_emb[None], (group_count, item_count, model_width)),
        "dp",
        split_axis=0,
        concat_axis=0,
        tiled=True,
    ).reshape(group_count * item_count, model_width)
    item_index = source * item_count + user_slot
    pick = (
        (item_index[:, None] == lax.broadcasted_iota(jnp.int32, (row_count, group_count * item_count), 1))
        & alive_mask
    ).astype(jnp.bfloat16)
    embedded = jnp.dot(pick, table, preferred_element_type=jnp.float32).astype(jnp.bfloat16)

    def normalize(vector):
        return rms_scale(vector, user_gain)

    scaled, norm_back = jax.vjp(normalize, embedded.astype(jnp.float32))
    hidden = scaled.astype(jnp.bfloat16)
    hidden_cols = lax.all_to_all(hidden, "fsdp", split_axis=1, concat_axis=0, tiled=True)
    gathered, hidden_cols = lax.optimization_barrier((gathered, hidden_cols))
    weights = gathered[:, :shard_rows].reshape(fsdp_count * shard_rows, key_weight.shape[1])
    grads_all = gathered[:, shard_rows:].reshape(fsdp_count * key_grad.shape[0], key_grad.shape[1])
    key_rows = jnp.dot(hidden, weights, preferred_element_type=jnp.float32).astype(jnp.bfloat16)
    hidden_grad = lax.dot_general(
        key_grad, weights, (((1,), (1,)), ((), ())), preferred_element_type=jnp.float32
    )
    (embed_grad,) = norm_back(hidden_grad)
    pos_grad = jnp.where(alive_mask, embed_grad, jnp.zeros_like(embed_grad)).astype(jnp.bfloat16)
    weight_part = lax.dot_general(
        hidden_cols, grads_all, (((0,), (0,)), ((), ())), preferred_element_type=jnp.float32
    )
    weight_rows, weight_cols = weight_part.shape
    item_part = lax.dot_general(
        pick, pos_grad, (((0,), (0,)), ((), ())), preferred_element_type=jnp.float32
    )
    item_rows = item_count * model_width // weight_cols
    outgoing = jnp.concatenate(
        [
            weight_part.reshape(group_count, weight_rows // group_count, weight_cols),
            item_part.reshape(group_count, item_rows, weight_cols),
        ],
        axis=1,
    ).astype(jnp.bfloat16)
    arrived = jnp.sum(
        lax.all_to_all(outgoing, "dp", split_axis=0, concat_axis=0, tiled=True).astype(jnp.float32), axis=0
    )
    reduced = arrived[: weight_rows // group_count]
    item_grad = arrived[weight_rows // group_count :].reshape(item_count, model_width)
    weight_grad = lax.all_to_all(
        jnp.broadcast_to(reduced[None], (group_count,) + reduced.shape),
        "dp",
        split_axis=0,
        concat_axis=0,
        tiled=True,
    ).reshape(weight_rows, weight_cols)
    (tokens_back,) = pool_back(item_grad)
    token_grads = tokens_back.reshape(item_count * block_rows, model_width).astype(jnp.bfloat16)
    return (key_rows, weight_grad, token_grads)


def solution(mesh):
    in_specs = (
        P(("dp", "fsdp"), None),
        P(("dp", "fsdp")),
        P(),
        P(("dp", "fsdp"), None),
        P(("dp", "fsdp")),
        P(("dp", "fsdp")),
        P(),
        P("fsdp", None),
        P(("dp", "fsdp"), None),
    )
    out_specs = (P(("dp", "fsdp"), None), P("fsdp", None), P(("dp", "fsdp"), None))
    return jax.shard_map(local, mesh=mesh, in_specs=in_specs, out_specs=out_specs, check_vma=False)
```

```python
import jax
import jax.numpy as jnp
from jax import lax
from jax.sharding import PartitionSpec as P

EPS = 1e-05


def rms_scale(vector, gain_row):
    return vector * lax.rsqrt(jnp.mean(vector * vector, axis=-1, keepdims=True) + EPS) * gain_row


def pool_items(token_block, valid_mask, item_sizes, gain_row):
    normed = rms_scale(token_block, gain_row)
    return jnp.sum(normed * valid_mask[:, :, None], axis=1) / item_sizes[:, None]


def local(
    item_tokens,
    item_lengths,
    item_gain,
    user_source,
    user_slot,
    user_lengths,
    user_gain,
    key_weight,
    key_grad,
):
    item_count = item_lengths.shape[0]
    block_rows = item_tokens.shape[0] // item_count
    model_width = item_tokens.shape[1]
    group_count = lax.axis_size("dp")
    stacked_tokens = item_tokens.reshape(item_count, block_rows, model_width)
    valid_mask = (
        lax.broadcasted_iota(jnp.int32, (item_count, block_rows), 1) < item_lengths[:, None]
    ).astype(jnp.float32)
    item_sizes = item_lengths.astype(jnp.float32)

    def pooling(tokens_float):
        return pool_items(tokens_float, valid_mask, item_sizes, item_gain)

    pooled, pool_back = jax.vjp(pooling, stacked_tokens.astype(jnp.float32))
    item_emb = pooled.astype(jnp.bfloat16)
    fsdp_count = lax.axis_size("fsdp")
    shard_rows = key_weight.shape[0]
    gathered = lax.all_gather(
        jnp.concatenate([key_weight, key_grad], axis=0), "fsdp", axis=0, tiled=False
    )
    row_count = user_slot.shape[0]
    source = user_source[:, 0]
    seq_count = user_lengths.shape[0]
    seq_rows = row_count // seq_count
    alive_mask = (
        lax.broadcasted_iota(jnp.int32, (seq_count, seq_rows), 1) < user_lengths[:, None]
    ).reshape(row_count, 1)
    table = lax.all_to_all(
        jnp.broadcast_to(item_emb[None], (group_count, item_count, model_width)),
        "dp",
        split_axis=0,
        concat_axis=0,
        tiled=True,
    ).reshape(group_count * item_count, model_width)
    item_index = source * item_count + user_slot
    pick = (
        (item_index[:, None] == lax.broadcasted_iota(jnp.int32, (row_count, group_count * item_count), 1))
        & alive_mask
    ).astype(jnp.bfloat16)
    embedded = jnp.dot(pick, table, preferred_element_type=jnp.float32).astype(jnp.bfloat16)

    def normalize(vector):
        return rms_scale(vector, user_gain)

    scaled, norm_back = jax.vjp(normalize, embedded.astype(jnp.float32))
    hidden = scaled.astype(jnp.bfloat16)
    hidden_cols = lax.all_to_all(hidden, "fsdp", split_axis=1, concat_axis=0, tiled=True)
    gathered, hidden_cols = lax.optimization_barrier((gathered, hidden_cols))
    weights = gathered[:, :shard_rows]
    grads_all = gathered[:, shard_rows:]
    hidden_blocks = hidden.reshape(row_count, fsdp_count, shard_rows)
    key_rows = lax.dot_general(
        hidden_blocks, weights, (((1, 2), (0, 1)), ((), ())), preferred_element_type=jnp.float32
    ).astype(jnp.bfloat16)
    hidden_grad = lax.dot_general(
        key_grad, weights, (((1,), (2,)), ((), ())), preferred_element_type=jnp.float32
    ).reshape(row_count, model_width)
    (embed_grad,) = norm_back(hidden_grad)
    pos_grad = jnp.where(alive_mask, embed_grad, jnp.zeros_like(embed_grad)).astype(jnp.bfloat16)
    weight_part = lax.dot_general(
        hidden_cols.reshape(grads_all.shape[0], grads_all.shape[1], shard_rows),
        grads_all,
        (((0, 1), (0, 1)), ((), ())),
        preferred_element_type=jnp.float32,
    )
    weight_rows, weight_cols = weight_part.shape
    item_part = lax.dot_general(
        pick, pos_grad, (((0,), (0,)), ((), ())), preferred_element_type=jnp.float32
    )
    item_rows = item_count * model_width // weight_cols
    outgoing = jnp.concatenate(
        [
            weight_part.reshape(group_count, weight_rows // group_count, weight_cols),
            item_part.reshape(group_count, item_rows, weight_cols),
        ],
        axis=1,
    ).astype(jnp.bfloat16)
    arrived = jnp.sum(
        lax.all_to_all(outgoing, "dp", split_axis=0, concat_axis=0, tiled=True).astype(jnp.float32), axis=0
    )
    reduced = arrived[: weight_rows // group_count]
    item_grad = arrived[weight_rows // group_count :].reshape(item_count, model_width)
    weight_grad = lax.all_to_all(
        jnp.broadcast_to(reduced[None], (group_count,) + reduced.shape),
        "dp",
        split_axis=0,
        concat_axis=0,
        tiled=True,
    ).reshape(weight_rows, weight_cols)
    (tokens_back,) = pool_back(item_grad)
    token_grads = tokens_back.reshape(item_count * block_rows, model_width).astype(jnp.bfloat16)
    return (key_rows, weight_grad, token_grads)


def solution(mesh):
    in_specs = (
        P(("dp", "fsdp"), None),
        P(("dp", "fsdp")),
        P(),
        P(("dp", "fsdp"), None),
        P(("dp", "fsdp")),
        P(("dp", "fsdp")),
        P(),
        P("fsdp", None),
        P(("dp", "fsdp"), None),
    )
    out_specs = (P(("dp", "fsdp"), None), P("fsdp", None), P(("dp", "fsdp"), None))
    return jax.shard_map(local, mesh=mesh, in_specs=in_specs, out_specs=out_specs, check_vma=False)
```

```python
import jax
import jax.numpy as jnp
from jax import lax
from jax.sharding import PartitionSpec as P

EPS = 1e-05


def rms_scale(vector, gain_row):
    return vector * lax.rsqrt(jnp.mean(vector * vector, axis=-1, keepdims=True) + EPS) * gain_row


def pool_items(token_block, valid_mask, item_sizes, gain_row):
    normed = rms_scale(token_block, gain_row)
    return jnp.sum(normed * valid_mask[:, :, None], axis=1) / item_sizes[:, None]


def local(
    item_tokens,
    item_lengths,
    item_gain,
    user_source,
    user_slot,
    user_lengths,
    user_gain,
    key_weight,
    key_grad,
):
    item_count = item_lengths.shape[0]
    block_rows = item_tokens.shape[0] // item_count
    model_width = item_tokens.shape[1]
    group_count = lax.axis_size("dp")
    stacked_tokens = item_tokens.reshape(item_count, block_rows, model_width)
    valid_mask = (
        lax.broadcasted_iota(jnp.int32, (item_count, block_rows), 1) < item_lengths[:, None]
    ).astype(jnp.float32)
    item_sizes = item_lengths.astype(jnp.float32)

    def pooling(tokens_float):
        return pool_items(tokens_float, valid_mask, item_sizes, item_gain)

    pooled, pool_back = jax.vjp(pooling, stacked_tokens.astype(jnp.float32))
    item_emb = pooled.astype(jnp.bfloat16)
    fsdp_count = lax.axis_size("fsdp")
    shard_rows = key_weight.shape[0]
    gathered = lax.all_gather(
        jnp.concatenate([key_weight, key_grad], axis=0), "fsdp", axis=0, tiled=False
    )
    row_count = user_slot.shape[0]
    source = user_source[:, 0]
    seq_count = user_lengths.shape[0]
    seq_rows = row_count // seq_count
    alive_mask = (
        lax.broadcasted_iota(jnp.int32, (seq_count, seq_rows), 1) < user_lengths[:, None]
    ).reshape(row_count, 1)
    table = lax.all_to_all(
        jnp.broadcast_to(item_emb[None], (group_count, item_count, model_width)),
        "dp",
        split_axis=0,
        concat_axis=0,
        tiled=True,
    ).reshape(group_count * item_count, model_width)
    item_index = source * item_count + user_slot
    pick = (
        (item_index[:, None] == lax.broadcasted_iota(jnp.int32, (row_count, group_count * item_count), 1))
        & alive_mask
    ).astype(jnp.bfloat16)
    embedded = jnp.dot(pick, table, preferred_element_type=jnp.float32).astype(jnp.bfloat16)

    def normalize(vector):
        return rms_scale(vector, user_gain)

    scaled, norm_back = jax.vjp(normalize, embedded.astype(jnp.float32))
    hidden = scaled.astype(jnp.bfloat16)
    hidden_cols = lax.all_to_all(hidden, "fsdp", split_axis=1, concat_axis=0, tiled=True)
    gathered, hidden_cols = lax.optimization_barrier((gathered, hidden_cols))
    weights = gathered[:, :shard_rows].reshape(fsdp_count * shard_rows, key_weight.shape[1])
    grads_all = gathered[:, shard_rows:].reshape(fsdp_count * key_grad.shape[0], key_grad.shape[1])
    key_rows = jnp.dot(hidden, weights, preferred_element_type=jnp.float32).astype(jnp.bfloat16)
    hidden_grad = lax.dot_general(
        key_grad, weights, (((1,), (1,)), ((), ())), preferred_element_type=jnp.float32
    )
    (embed_grad,) = norm_back(hidden_grad)
    pos_grad = jnp.where(alive_mask, embed_grad, jnp.zeros_like(embed_grad)).astype(jnp.bfloat16)
    weight_part = lax.dot_general(
        hidden_cols, grads_all, (((0,), (0,)), ((), ())), preferred_element_type=jnp.float32
    )
    weight_rows, weight_cols = weight_part.shape
    item_part = lax.dot_general(
        pick, pos_grad, (((0,), (0,)), ((), ())), preferred_element_type=jnp.float32
    )
    item_rows = item_count * model_width // weight_cols
    outgoing = jnp.concatenate(
        [
            weight_part.reshape(group_count, weight_rows // group_count, weight_cols),
            item_part.reshape(group_count, item_rows, weight_cols),
        ],
        axis=1,
    ).astype(jnp.bfloat16)
    arrived = jnp.sum(
        lax.all_to_all(outgoing, "dp", split_axis=0, concat_axis=0, tiled=True).astype(jnp.float32), axis=0
    )
    reduced = arrived[: weight_rows // group_count]
    item_grad = arrived[weight_rows // group_count :].reshape(item_count, model_width)
    weight_grad = (
        lax.all_to_all(
            jnp.broadcast_to(reduced.astype(jnp.bfloat16)[None], (group_count,) + reduced.shape),
            "dp",
            split_axis=0,
            concat_axis=0,
            tiled=True,
        )
        .reshape(weight_rows, weight_cols)
        .astype(jnp.float32)
    )
    (tokens_back,) = pool_back(item_grad)
    token_grads = tokens_back.reshape(item_count * block_rows, model_width).astype(jnp.bfloat16)
    return (key_rows, weight_grad, token_grads)


def solution(mesh):
    in_specs = (
        P(("dp", "fsdp"), None),
        P(("dp", "fsdp")),
        P(),
        P(("dp", "fsdp"), None),
        P(("dp", "fsdp")),
        P(("dp", "fsdp")),
        P(),
        P("fsdp", None),
        P(("dp", "fsdp"), None),
    )
    out_specs = (P(("dp", "fsdp"), None), P("fsdp", None), P(("dp", "fsdp"), None))
    return jax.shard_map(local, mesh=mesh, in_specs=in_specs, out_specs=out_specs, check_vma=False)
```

```python
import jax
import jax.numpy as jnp
from jax import lax
from jax.sharding import PartitionSpec as P

EPS = 1e-05


def rms_scale(vector, gain_row):
    return vector * lax.rsqrt(jnp.mean(vector * vector, axis=-1, keepdims=True) + EPS) * gain_row


def pool_items(token_block, valid_mask, item_sizes, gain_row):
    normed = rms_scale(token_block, gain_row)
    return jnp.sum(normed * valid_mask[:, :, None], axis=1) / item_sizes[:, None]


def local(
    item_tokens,
    item_lengths,
    item_gain,
    user_source,
    user_slot,
    user_lengths,
    user_gain,
    key_weight,
    key_grad,
):
    item_count = item_lengths.shape[0]
    block_rows = item_tokens.shape[0] // item_count
    model_width = item_tokens.shape[1]
    group_count = lax.axis_size("dp")
    stacked_tokens = item_tokens.reshape(item_count, block_rows, model_width)
    valid_mask = (
        lax.broadcasted_iota(jnp.int32, (item_count, block_rows), 1) < item_lengths[:, None]
    ).astype(jnp.float32)
    item_sizes = item_lengths.astype(jnp.float32)

    def pooling(tokens_float):
        return pool_items(tokens_float, valid_mask, item_sizes, item_gain)

    pooled, pool_back = jax.vjp(pooling, stacked_tokens.astype(jnp.float32))
    item_emb = pooled.astype(jnp.bfloat16)
    fsdp_count = lax.axis_size("fsdp")
    shard_rows = key_weight.shape[0]
    gathered = lax.all_gather(
        jnp.concatenate([key_weight, key_grad], axis=0), "fsdp", axis=0, tiled=False
    )
    row_count = user_slot.shape[0]
    source = user_source[:, 0]
    seq_count = user_lengths.shape[0]
    seq_rows = row_count // seq_count
    alive_mask = (
        lax.broadcasted_iota(jnp.int32, (seq_count, seq_rows), 1) < user_lengths[:, None]
    ).reshape(row_count, 1)
    table = lax.all_to_all(
        jnp.broadcast_to(item_emb[None], (group_count, item_count, model_width)),
        "dp",
        split_axis=0,
        concat_axis=0,
        tiled=True,
    ).reshape(group_count * item_count, model_width)
    item_index = source * item_count + user_slot
    pick = (
        (item_index[:, None] == lax.broadcasted_iota(jnp.int32, (row_count, group_count * item_count), 1))
        & alive_mask
    ).astype(jnp.bfloat16)
    embedded = jnp.dot(pick, table, preferred_element_type=jnp.float32).astype(jnp.bfloat16)

    def normalize(vector):
        return rms_scale(vector, user_gain)

    scaled, norm_back = jax.vjp(normalize, embedded.astype(jnp.float32))
    hidden = scaled.astype(jnp.bfloat16)
    hidden_cols = lax.all_to_all(hidden, "fsdp", split_axis=1, concat_axis=0, tiled=True)
    gathered, hidden_cols = lax.optimization_barrier((gathered, hidden_cols))
    weights = gathered[:, :shard_rows].reshape(fsdp_count * shard_rows, key_weight.shape[1])
    grads_all = gathered[:, shard_rows:].reshape(fsdp_count * key_grad.shape[0], key_grad.shape[1])
    key_rows = jnp.dot(hidden, weights, preferred_element_type=jnp.float32).astype(jnp.bfloat16)
    hidden_grad = lax.dot_general(
        key_grad, weights, (((1,), (1,)), ((), ())), preferred_element_type=jnp.float32
    )
    (embed_grad,) = norm_back(hidden_grad)
    pos_grad = jnp.where(alive_mask, embed_grad, jnp.zeros_like(embed_grad)).astype(jnp.bfloat16)
    weight_part = lax.dot_general(
        hidden_cols, grads_all, (((0,), (0,)), ((), ())), preferred_element_type=jnp.float32
    )
    weight_rows, weight_cols = weight_part.shape
    item_part = lax.dot_general(
        pick, pos_grad, (((0,), (0,)), ((), ())), preferred_element_type=jnp.float32
    )
    arrived = jnp.sum(
        lax.all_to_all(
            weight_part.reshape(group_count, weight_rows // group_count, weight_cols).astype(jnp.bfloat16),
            "dp",
            split_axis=0,
            concat_axis=0,
            tiled=True,
        ).astype(jnp.float32),
        axis=0,
    )
    reduced = arrived
    item_grad = jnp.sum(
        lax.all_to_all(
            item_part.reshape(group_count, item_count, model_width).astype(jnp.bfloat16),
            "dp",
            split_axis=0,
            concat_axis=0,
            tiled=True,
        ).astype(jnp.float32),
        axis=0,
    )
    weight_grad = (
        lax.all_to_all(
            jnp.broadcast_to(reduced.astype(jnp.bfloat16)[None], (group_count,) + reduced.shape),
            "dp",
            split_axis=0,
            concat_axis=0,
            tiled=True,
        )
        .reshape(weight_rows, weight_cols)
        .astype(jnp.float32)
    )
    (tokens_back,) = pool_back(item_grad)
    token_grads = tokens_back.reshape(item_count * block_rows, model_width).astype(jnp.bfloat16)
    return (key_rows, weight_grad, token_grads)


def solution(mesh):
    in_specs = (
        P(("dp", "fsdp"), None),
        P(("dp", "fsdp")),
        P(),
        P(("dp", "fsdp"), None),
        P(("dp", "fsdp")),
        P(("dp", "fsdp")),
        P(),
        P("fsdp", None),
        P(("dp", "fsdp"), None),
    )
    out_specs = (P(("dp", "fsdp"), None), P("fsdp", None), P(("dp", "fsdp"), None))
    return jax.shard_map(local, mesh=mesh, in_specs=in_specs, out_specs=out_specs, check_vma=False)
```
